32 devices in a mesh: cell: 8 (over y, x, core), gene: 4 (over z).
Axes of the slice: x: 2, y: 2, z: 4, core: 2. Of those that a mesh axis runs over, the one named last changes fastest.
Arguments:
- counts: int32 [2048, 2560], P('cell', 'gene'), may hold values from 1 to 8
- cell_factors: float32 [64, 2048], P(None, 'cell'), may hold values from -6 to 6
- loadings: float32 [64, 2560], P(None, 'gene'), may hold values from -3 to 3
- cell_momenta: float32 [64, 2048], P(None, 'cell'), may hold values from -6 to 6
- loading_momenta: float32 [64, 2560], P(None, 'gene'), may hold values from -6 to 6
- step: float32 [64], replicated, may hold values from 0.01 to 0.04
Outputs:
- new_factors: float32 [64, 2048], P(None, 'cell')
- new_loadings: float32 [64, 2560], P(None, 'gene')
- new_cell_momenta: float32 [64, 2048], P(None, 'cell')
- new_loading_momenta: float32 [64, 2560], P(None, 'gene')
- log_rate: bfloat16 [2048, 2560], P('cell', 'gene')
The draws below stay inside these ranges and needn't reach their ends.
All inputs are finite; a program needn't handle non-finite values.
Results may differ from the reference program's by a relative error of at most 0.001.
Values sent between devices are 32-bit elements; how exact they have to be, the bound alone decides.
No kernel may reach another device: no remote copies, remote signals or barrier semaphores. Data moves between devices by JAX's collectives and lax.ppermute only.
A program may use at most 64 MiB of HBM per device.

```python
import math
import jax
import jax.numpy as jnp
from jax import lax

K = 64
CELL_DEV = 256
LEAPS = 1
CELLS = 2048
GENES = 2560
N_CELL = 8


def touch_ends(array, rng, least, high):
    longest = array.shape.index(max(array.shape))
    spots = []
    for shift in (0, 1):
        where = [jax.random.randint(jax.random.fold_in(rng, axis), (), 0, length) for axis, length in enumerate(array.shape)]
        where[longest] = (where[longest] + shift) % array.shape[longest]
        spots.append(tuple(where))
    return array.at[spots[0]].set(least).at[spots[1]].set(high)


def levels(stream_key, extent, shards, low, high):
    def one(dim, shards_of):
        draws = jax.random.uniform(jax.random.fold_in(jax.random.fold_in(stream_key, 6), dim), (shards_of,), jnp.float32, low / len(shards), high / len(shards))
        return jnp.repeat(jnp.exp(draws), extent[dim] // shards_of).reshape((-1,) + (1,) * (len(extent) - dim - 1))

    loudness = one(*shards[0])
    for cut in shards[1:]:
        loudness = loudness * one(*cut)
    return loudness


def gaussian(rng, extent, scale, reach, cuts=(), kind=jnp.bfloat16):
    drawn = jax.random.normal(rng, extent, jnp.float32) * scale
    if len(cuts) > 0:
        drawn = levels(rng, extent, cuts, -0.22, 0.18) * drawn
    return jnp.clip(drawn, min=-reach, max=reach).astype(kind)


def setup_inputs(seed: int = 0) -> dict:
    seeds = jax.random.split(jax.random.key(seed), 7)
    return {
        "counts": touch_ends(jax.random.randint(seeds[0], (CELLS, GENES), 1, 9), jax.random.fold_in(seeds[0], 1), 1, 8).astype(jnp.int32),
        "cell_factors": gaussian(seeds[1], (K, CELLS), 1.0, 6.0, ((1, 8),), jnp.float32),
        "loadings": gaussian(seeds[2], (K, GENES), 0.5, 3.0, ((1, 4),), jnp.float32),
        "cell_momenta": gaussian(seeds[3], (K, CELLS), 1.0, 6.0, ((1, 8),), jnp.float32),
        "loading_momenta": gaussian(seeds[4], (K, GENES), 1.0, 6.0, ((1, 4),), jnp.float32),
        "step": jnp.clip(jnp.exp(jax.random.uniform(seeds[5], (K,), jnp.float32, math.log(0.01), math.log(0.04))), 0.01, 0.04),
    }


def gradient(factors, loadings, counts_float, library):
    scale = 1.0 / jnp.sqrt(jnp.float32(K))
    squares = lax.optimization_barrier(jnp.sum(loadings * loadings, axis=1))
    ard = (jnp.float32(GENES) + 2.0) / (squares + 2.0)
    blocks_u = jnp.transpose(factors.reshape(K, N_CELL, CELL_DEV), (1, 0, 2))
    blocks_y = counts_float.reshape(N_CELL, CELL_DEV, GENES)
    blocks_l = library.reshape(N_CELL, CELL_DEV)

    def one_block(carry, items):
        block_u, block_y, block_l = items
        linear = lax.dot_general(block_u, loadings, (((0,), (0,)), ((), ())), precision=lax.Precision.HIGHEST) * scale
        expo = jnp.exp(linear)
        total = lax.optimization_barrier(jnp.sum(expo, axis=1))
        size = block_l / total
        resid = block_y - size[:, None] * expo
        grad_u = lax.dot_general(loadings, resid, (((1,), (1,)), ((), ())), precision=lax.Precision.HIGHEST) * scale
        part_v = jnp.dot(block_u, resid, precision=lax.Precision.HIGHEST) * scale
        rates = (linear + jnp.log(size)[:, None]).astype(jnp.bfloat16)
        return (carry + part_v, (grad_u, rates))
    start = jnp.zeros((K, GENES), jnp.float32)
    part_v, (grad_u, rates) = lax.scan(one_block, start, (blocks_u, blocks_y, blocks_l))
    grad_u = jnp.transpose(grad_u, (1, 0, 2)).reshape(K, CELLS) - factors
    grad_v = part_v - ard[:, None] * loadings
    return (grad_u, grad_v, rates.reshape(CELLS, GENES))

def reference(counts, cell_factors, loadings, cell_momenta, loading_momenta, step):
    counts_float = counts.astype(jnp.float32)
    library = lax.optimization_barrier(jnp.sum(counts_float, axis=1))
    half = 0.5 * step[:, None]
    full = step[:, None]
    factors, loads = (cell_factors, loadings)
    mom_u, mom_v = (cell_momenta, loading_momenta)
    grad_u, grad_v, rates = gradient(factors, loads, counts_float, library)
    for leap in range(LEAPS):
        mom_u = mom_u + half * grad_u
        mom_v = mom_v + half * grad_v
        factors = factors + full * mom_u
        loads = loads + full * mom_v
        grad_u, grad_v, rates = gradient(factors, loads, counts_float, library)
        mom_u = mom_u + half * grad_u
        mom_v = mom_v + half * grad_v
    return (factors, loads, mom_u, mom_v, rates)
```

```python
import jax
import jax.numpy as jnp
from jax import lax
from jax.sharding import PartitionSpec as P

K = 64
HIGH = lax.Precision.HIGHEST


def swap(x, axis, bits):
    n = lax.axis_size(axis)
    return lax.ppermute(x, axis, [(j, j ^ bits) for j in range(n)])


def stages(lo, n):
    out = []
    bit = lo
    while bit < n:
        out.append([bit, 2 * bit, 3 * bit] if 4 * bit <= n else [bit])
        bit *= 4
    return out


def exchange_sum(x, axis, lo):
    for group in stages(lo, lax.axis_size(axis)):
        parts = [swap(x, axis, bits) for bits in group]
        for part in parts:
            x = x + part
    return x


def local(counts, cell_factors, loadings, cell_momenta, loading_momenta, step):
    scale = 1.0 / jnp.sqrt(jnp.float32(K))
    counts_float = counts.astype(jnp.float32)
    genes_total = jnp.float32(loadings.shape[1] * lax.axis_size("gene"))
    cells = cell_factors.shape[1]
    hk = K // 2
    side = lax.axis_index("cell") % 2

    def mine(x):
        return lax.dynamic_slice_in_dim(x, side * hk, hk, 0)

    def other(x):
        return lax.dynamic_slice_in_dim(x, (1 - side) * hk, hk, 0)

    def join(x):
        y = swap(x, "cell", 1)
        first = side == 0
        return jnp.concatenate([jnp.where(first, x, y), jnp.where(first, y, x)], 0)

    half = 0.5 * step[:, None]
    full = step[:, None]
    half_own = mine(half)
    full_own = mine(full)

    def forward(factors, loads, extra):
        linear = (
            lax.dot_general(factors, loads, (((0,), (0,)), ((), ())), precision=HIGH) * scale
        )
        expo = jnp.exp(linear)
        pack = jnp.concatenate([jnp.sum(expo, axis=1), jnp.sum(loads * loads, axis=1)] + extra)
        return linear, expo, exchange_sum(pack, "gene", 1)

    def backward(factors, loads, own, expo, size, squares):
        resid = counts_float - size[:, None] * expo
        send = jnp.dot(other(factors), resid, precision=HIGH) * scale
        part = swap(send, "cell", 1)
        part = part + jnp.dot(mine(factors), resid, precision=HIGH) * scale
        part = exchange_sum(part, "cell", 2)
        cross = lax.dot_general(loads, resid, (((1,), (1,)), ((), ())), precision=HIGH) * scale
        cross = exchange_sum(cross, "gene", 1)
        ard = (genes_total + 2.0) / (squares + 2.0)
        grad_v = part - mine(ard[:, None]) * own
        return cross - factors, grad_v

    own = mine(loadings)
    mom_u = cell_momenta
    mom_v = mine(loading_momenta)
    factors = cell_factors
    library = jnp.sum(counts_float, axis=1)
    linear, expo, pack = forward(factors, loadings, [library])
    library = pack[cells + K :]
    size = library / pack[:cells]
    grad_u, grad_v = backward(factors, loadings, own, expo, size, pack[cells : cells + K])
    mom_u = mom_u + half * grad_u
    mom_v = mom_v + half_own * grad_v
    factors = factors + full * mom_u
    own = own + full_own * mom_v
    loads = join(own)
    linear, expo, pack = forward(factors, loads, [])
    size = library / pack[:cells]
    grad_u, grad_v = backward(factors, loads, own, expo, size, pack[cells : cells + K])
    mom_u = mom_u + half * grad_u
    mom_v = join(mom_v + half_own * grad_v)
    rates = (linear + jnp.log(size)[:, None]).astype(jnp.bfloat16)
    return (factors, loads, mom_u, mom_v, rates)


def solution(mesh):
    placed = (
        P("cell", "gene"),
        P(None, "cell"),
        P(None, "gene"),
        P(None, "cell"),
        P(None, "gene"),
        P(),
    )
    return jax.shard_map(
        local,
        mesh=mesh,
        in_specs=placed,
        out_specs=(
            P(None, "cell"),
            P(None, "gene"),
            P(None, "cell"),
            P(None, "gene"),
            P("cell", "gene"),
        ),
        check_vma=False,
    )
```

```python
import functools

import jax
import jax.numpy as jnp
from jax import lax
from jax.experimental import pallas as pl
from jax.experimental.pallas import tpu as pltpu
from jax.sharding import PartitionSpec as P


PARAMS = pltpu.CompilerParams(vmem_limit_bytes=24 * 1024 * 1024)
PIECES = 4
FLOOR = 2.0**-100
VMEM = pl.BlockSpec(memory_space=pltpu.VMEM)
SMEM = pl.BlockSpec(memory_space=pltpu.SMEM)
NT = (((1,), (1,)), ((), ()))
TN = (((0,), (0,)), ((), ()))
NN = (((1,), (0,)), ((), ()))


def dot(a, b, dims):
    return lax.dot_general(a, b, dims, preferred_element_type=jnp.float32)


def split(x):
    high = x.astype(jnp.bfloat16)
    return high, (x - high.astype(jnp.float32)).astype(jnp.bfloat16)


def weight_of(total):
    return jnp.maximum(0.25 * total, FLOOR)


def forward_math(scale, u, v, counts_of, wide_ref, pack_ref, high_ref, low_ref):
    k = u.shape[0]
    u_high, u_low = split(u * scale)
    v_high, v_low = split(v)
    linear = dot(
        jnp.concatenate([v_high, v_low, v_high, v_low], 0),
        jnp.concatenate([u_high, u_high, u_low, u_low], 0),
        TN,
    )
    expo = jnp.exp(linear)
    total = jnp.sum(expo, axis=0, keepdims=True)
    prob = expo * (1.0 / weight_of(total))
    p_high, p_low = split(prob)
    high_ref[...] = p_high
    low_ref[...] = p_low
    w_high, w_low = split(v * scale)
    mean = dot(jnp.concatenate([w_high, w_low], 0), p_high, NN)
    wide_ref[k : 2 * k, :] = mean[:k] + mean[k:] + dot(w_high, p_low, NN)
    ones = jnp.ones((16, v.shape[1]), jnp.bfloat16)
    s_high, s_low = split(v * v)
    squares = dot(ones, s_high, NT) + dot(ones, s_low, NT)
    data = dot(jnp.concatenate([w_high, w_low, ones], 0), counts_of(), NT)
    wide_ref[0:k, :] = data[:k] + data[k : 2 * k]
    for ref, at in ((wide_ref, 2 * k), (pack_ref, 0)):
        ref[at : at + 8, :] = jnp.zeros((8, pack_ref.shape[1]), jnp.float32)
        ref[at : at + 1, :] = total
        ref[at + 1 : at + 2, :] = data[2 * k : 2 * k + 1]
        ref[at + 2 : at + 3, 0:k] = squares[0:1]


def first_kernel(scale, counts_hbm, u_hbm, v_hbm, wide_ref, pack_ref, high_ref, low_ref, small_ref,
                 counts_ref, u_ref, v_ref, sems):
    copies = [
        pltpu.make_async_copy(u_hbm, u_ref, sems.at[0]),
        pltpu.make_async_copy(v_hbm, v_ref, sems.at[1]),
    ]
    pieces = sems.shape[0] - 2
    rows = counts_ref.shape[0] // pieces
    for i in range(pieces):
        at = pl.ds(i * rows, rows)
        copies.append(
            pltpu.make_async_copy(counts_hbm.at[at, :], counts_ref.at[at, :], sems.at[2 + i])
        )
    for copy in copies:
        copy.start()
    copies[0].wait()
    copies[1].wait()

    def counts_of():
        for copy in copies[2:]:
            copy.wait()
        small = counts_ref[...].astype(jnp.float32).astype(jnp.bfloat16)
        small_ref[...] = small
        return small

    forward_math(
        scale, u_ref[...], v_ref[...], counts_of, wide_ref, pack_ref, high_ref, low_ref
    )


def again_kernel(scale, counts_ref, u_ref, v_ref, *outs):
    forward_math(scale, u_ref[...], v_ref[...], lambda: counts_ref[...], *outs)


def forward(counts, u, v, scale, first):
    k, cells = u.shape
    genes = v.shape[1]
    shapes = [
        jax.ShapeDtypeStruct((2 * k + 8, cells), jnp.float32),
        jax.ShapeDtypeStruct((8, cells), jnp.float32),
        jax.ShapeDtypeStruct((genes, cells), jnp.bfloat16),
        jax.ShapeDtypeStruct((genes, cells), jnp.bfloat16),
    ]
    if not first:
        return pl.pallas_call(
            functools.partial(again_kernel, scale),
            out_shape=shapes,
            in_specs=[VMEM] * 3,
            out_specs=[VMEM] * len(shapes),
            name="forward_again",
            compiler_params=PARAMS,
        )(counts, u, v)
    shapes.append(jax.ShapeDtypeStruct((cells, genes), jnp.bfloat16))
    pieces = PIECES
    return pl.pallas_call(
        functools.partial(first_kernel, scale),
        out_shape=shapes,
        in_specs=[pl.BlockSpec(memory_space=pltpu.HBM)] * 3,
        out_specs=[VMEM] * len(shapes),
        scratch_shapes=[
            pltpu.VMEM((cells, genes), counts.dtype),
            pltpu.VMEM(u.shape, u.dtype),
            pltpu.VMEM(v.shape, v.dtype),
            pltpu.SemaphoreType.DMA((2 + pieces,)),
        ],
        name="forward_first",
        compiler_params=PARAMS,
    )(counts, u, v)


def rates_kernel(scale, u_ref, v_ref, size_ref, out_ref):
    u_high, u_low = split(u_ref[...] * scale)
    v_high, v_low = split(v_ref[...])
    linear = dot(
        jnp.concatenate([u_high, u_high, u_low, u_low], 0),
        jnp.concatenate([v_high, v_low, v_high, v_low], 0),
        TN,
    )
    log = jnp.log(size_ref[...])
    log_high, log_low = split(log)
    log_least = (log - log_high.astype(jnp.float32) - log_low.astype(jnp.float32)).astype(
        jnp.bfloat16
    )
    row = lax.broadcasted_iota(jnp.int32, (16, log.shape[1]), 0)
    terms = jnp.zeros((16, log.shape[1]), jnp.float32)
    for i, term in enumerate((log_high, log_low, log_least)):
        terms = jnp.where(row == i, term.astype(jnp.float32), terms)
    ones = jnp.ones((16, v_ref.shape[1]), jnp.bfloat16)
    shift = dot(terms.astype(jnp.bfloat16), ones, TN)
    out_ref[...] = (linear + shift).astype(jnp.bfloat16)


def rates_of(u, v, size, scale):
    return pl.pallas_call(
        functools.partial(rates_kernel, scale),
        out_shape=jax.ShapeDtypeStruct((u.shape[1], v.shape[1]), jnp.bfloat16),
        in_specs=[VMEM] * 3,
        out_specs=VMEM,
        name="rates",
        compiler_params=PARAMS,
    )(u, v, size)


def data_kernel(scale, counts_ref, u_ref, out_ref):
    k = u_ref.shape[0]
    u_high, u_low = split(u_ref[...] * scale)
    both = dot(jnp.concatenate([u_high, u_low], 0), counts_ref[...], NN)
    out_ref[...] = both[:k] + both[k:]


def data_part(counts, u, scale):
    return pl.pallas_call(
        functools.partial(data_kernel, scale),
        out_shape=jax.ShapeDtypeStruct((u.shape[0], counts.shape[1]), jnp.float32),
        in_specs=[VMEM] * 2,
        out_specs=VMEM,
        name="data_part",
        compiler_params=PARAMS,
    )(counts, u)


def part_kernel(scale, at_ref, u_ref, size_ref, data_ref, high_ref, low_ref, out_ref):
    hk = out_ref.shape[0]
    rows = pl.ds(pl.multiple_of(at_ref[0], hk), hk)
    u_high, u_low = split(u_ref[rows, :] * size_ref[...] * scale)
    both = dot(jnp.concatenate([u_high, u_low], 0), high_ref[...], NT)
    rest = dot(u_high, low_ref[...], NT)
    out_ref[...] = data_ref[rows, :] - (both[:hk] + both[hk:] + rest)


def part(at, u, size, data, high, low, scale):
    return pl.pallas_call(
        functools.partial(part_kernel, scale),
        out_shape=jax.ShapeDtypeStruct((u.shape[0] // 2, high.shape[0]), jnp.float32),
        in_specs=[SMEM] + [VMEM] * 5,
        out_specs=VMEM,
        compiler_params=PARAMS,
    )(at, u, size, data, high, low)


def swap(x, axis, bits):
    n = lax.axis_size(axis)
    return lax.ppermute(x, axis, [(j, j ^ bits) for j in range(n)])


def stages(lo, n):
    out = []
    bit = lo
    while bit < n:
        out.append([bit, 2 * bit, 3 * bit] if 4 * bit <= n else [bit])
        bit *= 4
    return out


def exchange_sum(x, axis, lo):
    for group in stages(lo, lax.axis_size(axis)):
        parts = [swap(x, axis, bits) for bits in group]
        for got in parts:
            x = x + got
    return x


def local(counts, cell_factors, loadings, cell_momenta, loading_momenta, step):
    k, _ = cell_factors.shape
    scale = 1.0 / k**0.5
    n_gene = lax.axis_size("gene")
    genes_total = jnp.float32(loadings.shape[1] * n_gene)
    hk = k // 2
    side = lax.axis_index("cell") % 2
    at_own = jnp.reshape(side * hk, (1,)).astype(jnp.int32)
    at_send = hk - at_own

    def mine(x):
        return lax.dynamic_slice_in_dim(x, side * hk, hk, 0)

    def join(x):
        y = swap(x, "cell", 1)
        first = side == 0
        return jnp.concatenate([jnp.where(first, x, y), jnp.where(first, y, x)], 0)

    half = 0.5 * step[:, None]
    full = step[:, None]
    half_own = mine(half)
    full_own = mine(full)

    def gather(wide, pack):
        got = swap(wide, "gene", 1)
        narrow = [swap(pack, "gene", bits) for bits in stages(1, n_gene)[0][1:]]
        near = got[2 * k :]
        whole = pack + near
        for more in narrow:
            whole = whole + more
        if n_gene > 4:
            whole = exchange_sum(whole, "gene", 4)
        return got, near, whole

    def cross_of(wide, got, pack, near, size):
        own_size = size * weight_of(pack[0:1])
        near_size = size * weight_of(near[0:1])
        cross = (wide[:k] + got[:k]) - own_size * wide[k : 2 * k] - near_size * got[k : 2 * k]
        bit = 2
        while bit < n_gene:
            cross = cross + swap(cross, "gene", bit)
            bit *= 2
        return cross, own_size

    def gradient(counts_in, factors, loads, own, library, first):
        wide, pack, high, low, *rest = forward(counts_in, factors, loads, scale, first)
        counts_in = rest[0] if first else counts_in
        got, near, whole = gather(wide, pack)
        data = data_part(counts_in, factors, scale)
        library = whole[1:2] if first else library
        size = library / whole[0:1]
        cross, own_size = cross_of(wide, got, pack, near, size)
        send = part(at_send, factors, own_size, data, high, low, scale)
        back = swap(send, "cell", 1)
        kept = part(at_own, factors, own_size, data, high, low, scale)
        total = exchange_sum(back + kept, "cell", 2)
        ard = (genes_total + 2.0) / (whole[2, :k] + 2.0)
        return cross - factors, total - mine(ard[:, None]) * own, library, size, counts_in

    own = mine(loadings)
    mom_v = mine(loading_momenta)
    grad_u, grad_v, library, size, counts_small = gradient(
        counts, cell_factors, loadings, own, None, True
    )
    mom_u = cell_momenta + half * grad_u
    mom_v = mom_v + half_own * grad_v
    factors = cell_factors + full * mom_u
    own = own + full_own * mom_v
    loads = join(own)
    grad_u, grad_v, library, size, _ = gradient(counts_small, factors, loads, own, library, False)
    rates = rates_of(factors, loads, size, scale)
    mom_u = mom_u + half * grad_u
    mom_v = join(mom_v + half_own * grad_v)
    return (factors, loads, mom_u, mom_v, rates)


def solution(mesh):
    placed = (
        P("cell", "gene"),
        P(None, "cell"),
        P(None, "gene"),
        P(None, "cell"),
        P(None, "gene"),
        P(),
    )
    return jax.shard_map(
        local,
        mesh=mesh,
        in_specs=placed,
        out_specs=(
            P(None, "cell"),
            P(None, "gene"),
            P(None, "cell"),
            P(None, "gene"),
            P("cell", "gene"),
        ),
        check_vma=False,
    )
```

```python
import functools

import jax
import jax.numpy as jnp
from jax import lax
from jax.experimental import pallas as pl
from jax.experimental.pallas import tpu as pltpu
from jax.sharding import PartitionSpec as P


PARAMS = pltpu.CompilerParams(vmem_limit_bytes=24 * 1024 * 1024)
PIECES = 4
FLOOR = 2.0**-100
VMEM = pl.BlockSpec(memory_space=pltpu.VMEM)
HBM = pl.BlockSpec(memory_space=pltpu.HBM)
SMEM = pl.BlockSpec(memory_space=pltpu.SMEM)
NT = (((1,), (1,)), ((), ()))
TN = (((0,), (0,)), ((), ()))
NN = (((1,), (0,)), ((), ()))


def dot(a, b, dims):
    return lax.dot_general(a, b, dims, preferred_element_type=jnp.float32)


def split(x):
    high = x.astype(jnp.bfloat16)
    return high, (x - high.astype(jnp.float32)).astype(jnp.bfloat16)


def weight_of(total):
    return jnp.clip(0.25 * total, FLOOR, 2.0**126)


def forward_math(scale, u, v, pack_ref, high_ref, low_ref):
    u_high, u_low = split(u * scale)
    v_high, v_low = split(v)
    linear = dot(
        jnp.concatenate([v_high, v_low, v_high, v_low], 0),
        jnp.concatenate([u_high, u_high, u_low, u_low], 0),
        TN,
    )
    expo = jnp.exp(linear)
    total = jnp.sum(expo, axis=0, keepdims=True)
    p_high, p_low = split(expo * (1.0 / weight_of(total)))
    high_ref[...] = p_high
    low_ref[...] = p_low
    ones = jnp.ones((16, v.shape[1]), jnp.bfloat16)
    s_high, s_low = split(v * v)
    squares = dot(ones, s_high, NT) + dot(ones, s_low, NT)
    pack_ref[...] = jnp.zeros(pack_ref.shape, jnp.float32)
    pack_ref[0:1, :] = total
    pack_ref[2:3, 0 : v.shape[0]] = squares[0:1]


def first_kernel(scale, counts_hbm, u_hbm, v_hbm, step_hbm, pack_ref, high_ref, low_ref, small_ref,
                 u_ref, v_ref, step_ref, counts_ref, sems):
    copies = [
        pltpu.make_async_copy(v_hbm, v_ref, sems.at[0]),
        pltpu.make_async_copy(u_hbm, u_ref, sems.at[1]),
    ]
    pieces = sems.shape[0] - 3
    rows = counts_ref.shape[0] // pieces
    for i in range(pieces):
        at = pl.ds(i * rows, rows)
        copies.append(
            pltpu.make_async_copy(counts_hbm.at[at, :], counts_ref.at[at, :], sems.at[2 + i])
        )
    copies.append(pltpu.make_async_copy(step_hbm, step_ref, sems.at[2 + pieces]))
    for copy in copies:
        copy.start()
    copies[0].wait()
    copies[1].wait()
    forward_math(scale, u_ref[...], v_ref[...], pack_ref, high_ref, low_ref)
    for copy in copies[2:]:
        copy.wait()
    small = counts_ref[...].astype(jnp.float32).astype(jnp.bfloat16)
    small_ref[...] = small
    ones = jnp.ones((16, small.shape[1]), jnp.bfloat16)
    pack_ref[1:2, :] = dot(ones, small, NT)[0:1]


def again_kernel(scale, u_ref, v_ref, *outs):
    forward_math(scale, u_ref[...], v_ref[...], *outs)


def forward_first(counts, u, v, step, scale):
    cells, genes = counts.shape
    shapes = [
        jax.ShapeDtypeStruct((8, cells), jnp.float32),
        jax.ShapeDtypeStruct((genes, cells), jnp.bfloat16),
        jax.ShapeDtypeStruct((genes, cells), jnp.bfloat16),
        jax.ShapeDtypeStruct((cells, genes), jnp.bfloat16),
        jax.ShapeDtypeStruct(u.shape, u.dtype),
        jax.ShapeDtypeStruct(v.shape, v.dtype),
        jax.ShapeDtypeStruct(step.shape, step.dtype),
    ]
    return pl.pallas_call(
        functools.partial(first_kernel, scale),
        out_shape=shapes,
        in_specs=[HBM] * 4,
        out_specs=[VMEM] * len(shapes),
        scratch_shapes=[
            pltpu.VMEM((cells, genes), counts.dtype),
            pltpu.SemaphoreType.DMA((3 + PIECES,)),
        ],
        name="forward_first",
        compiler_params=PARAMS,
    )(*(pltpu.with_memory_space_constraint(x, pltpu.HBM) for x in (counts, u, v, step)))


def forward_again(u, v, scale):
    cells, genes = u.shape[1], v.shape[1]
    shapes = [
        jax.ShapeDtypeStruct((8, cells), jnp.float32),
        jax.ShapeDtypeStruct((genes, cells), jnp.bfloat16),
        jax.ShapeDtypeStruct((genes, cells), jnp.bfloat16),
    ]
    return pl.pallas_call(
        functools.partial(again_kernel, scale),
        out_shape=shapes,
        in_specs=[VMEM] * 2,
        out_specs=[VMEM] * len(shapes),
        name="forward_again",
        compiler_params=PARAMS,
    )(u, v)


def products_kernel(scale, counts_ref, v_ref, high_ref, low_ref, out_ref):
    k = v_ref.shape[0]
    w_high, w_low = split(v_ref[...] * scale)
    both = jnp.concatenate([w_high, w_low], 0)
    data = dot(both, counts_ref[...], NT)
    mean = dot(both, high_ref[...], NN)
    out_ref[0:k, :] = data[:k] + data[k:]
    out_ref[k:, :] = mean[:k] + mean[k:] + dot(w_high, low_ref[...], NN)


def products(counts, v, high, low, scale):
    return pl.pallas_call(
        functools.partial(products_kernel, scale),
        out_shape=jax.ShapeDtypeStruct((2 * v.shape[0], counts.shape[0]), jnp.float32),
        in_specs=[VMEM] * 4,
        out_specs=VMEM,
        name="products",
        compiler_params=PARAMS,
    )(counts, v, high, low)


def rates_kernel(scale, u_ref, v_ref, size_ref, out_ref):
    u_high, u_low = split(u_ref[...] * scale)
    v_high, v_low = split(v_ref[...])
    linear = dot(
        jnp.concatenate([u_high, u_high, u_low, u_low], 0),
        jnp.concatenate([v_high, v_low, v_high, v_low], 0),
        TN,
    )
    log = jnp.log(size_ref[...])
    log_high, log_low = split(log)
    log_least = (log - log_high.astype(jnp.float32) - log_low.astype(jnp.float32)).astype(
        jnp.bfloat16
    )
    row = lax.broadcasted_iota(jnp.int32, (16, log.shape[1]), 0)
    terms = jnp.zeros((16, log.shape[1]), jnp.float32)
    for i, term in enumerate((log_high, log_low, log_least)):
        terms = jnp.where(row == i, term.astype(jnp.float32), terms)
    ones = jnp.ones((16, v_ref.shape[1]), jnp.bfloat16)
    shift = dot(terms.astype(jnp.bfloat16), ones, TN)
    out_ref[...] = (linear + shift).astype(jnp.bfloat16)


def rates_of(u, v, size, scale):
    return pl.pallas_call(
        functools.partial(rates_kernel, scale),
        out_shape=jax.ShapeDtypeStruct((u.shape[1], v.shape[1]), jnp.bfloat16),
        in_specs=[VMEM] * 3,
        out_specs=VMEM,
        name="rates",
        compiler_params=PARAMS,
    )(u, v, size)


def data_kernel(scale, counts_ref, u_ref, out_ref):
    k = u_ref.shape[0]
    u_high, u_low = split(u_ref[...] * scale)
    both = dot(jnp.concatenate([u_high, u_low], 0), counts_ref[...], NN)
    out_ref[...] = both[:k] + both[k:]


def data_part(counts, u, scale):
    return pl.pallas_call(
        functools.partial(data_kernel, scale),
        out_shape=jax.ShapeDtypeStruct((u.shape[0], counts.shape[1]), jnp.float32),
        in_specs=[VMEM] * 2,
        out_specs=VMEM,
        name="data_part",
        compiler_params=PARAMS,
    )(counts, u)


def part_kernel(scale, at_ref, u_ref, size_ref, data_ref, high_ref, low_ref, out_ref):
    hk = out_ref.shape[0]
    rows = pl.ds(pl.multiple_of(at_ref[0], hk), hk)
    u_high, u_low = split(u_ref[rows, :] * size_ref[...] * scale)
    both = dot(jnp.concatenate([u_high, u_low], 0), high_ref[...], NT)
    rest = dot(u_high, low_ref[...], NT)
    out_ref[...] = data_ref[rows, :] - (both[:hk] + both[hk:] + rest)


def part(at, u, size, data, high, low, scale):
    return pl.pallas_call(
        functools.partial(part_kernel, scale),
        out_shape=jax.ShapeDtypeStruct((u.shape[0] // 2, high.shape[0]), jnp.float32),
        in_specs=[SMEM] + [VMEM] * 5,
        out_specs=VMEM,
        compiler_params=PARAMS,
    )(at, u, size, data, high, low)


def finish_kernel(at_ref, own_ref, other_ref, u_ref, u_hbm, v_hbm, sems):
    hk = own_ref.shape[0]
    first = pl.multiple_of(at_ref[0], hk)
    copies = (
        pltpu.make_async_copy(u_ref, u_hbm, sems.at[0]),
        pltpu.make_async_copy(own_ref, v_hbm.at[pl.ds(first, hk), :], sems.at[1]),
        pltpu.make_async_copy(other_ref, v_hbm.at[pl.ds(hk - first, hk), :], sems.at[2]),
    )
    for copy in copies:
        copy.start()
    for copy in copies:
        copy.wait()


def finish(at, own, other, u):
    hk, genes = own.shape
    return pl.pallas_call(
        finish_kernel,
        out_shape=(
            jax.ShapeDtypeStruct(u.shape, u.dtype),
            jax.ShapeDtypeStruct((2 * hk, genes), own.dtype),
        ),
        in_specs=[SMEM] + [VMEM] * 3,
        out_specs=(HBM, HBM),
        scratch_shapes=[pltpu.SemaphoreType.DMA((3,))],
        name="finish",
        compiler_params=PARAMS,
    )(at, own, other, u)


def swap(x, axis, bits):
    n = lax.axis_size(axis)
    return lax.ppermute(x, axis, [(j, j ^ bits) for j in range(n)])


def stages(lo, n):
    out = []
    bit = lo
    while bit < n:
        out.append([bit, 2 * bit, 3 * bit] if 4 * bit <= n else [bit])
        bit *= 4
    return out


def exchange_sum(x, axis, lo):
    for group in stages(lo, lax.axis_size(axis)):
        parts = [swap(x, axis, bits) for bits in group]
        for got in parts:
            x = x + got
    return x


def local(counts, cell_factors, loadings, cell_momenta, loading_momenta, step):
    k, _ = cell_factors.shape
    scale = 1.0 / k**0.5
    n_gene = lax.axis_size("gene")
    genes_total = jnp.float32(loadings.shape[1] * n_gene)
    hk = k // 2
    side = lax.axis_index("cell") % 2
    at_own = jnp.reshape(side * hk, (1,)).astype(jnp.int32)
    at_send = hk - at_own

    def mine(x):
        return lax.dynamic_slice_in_dim(x, side * hk, hk, 0)

    def join(x):
        y = swap(x, "cell", 1)
        first = side == 0
        return jnp.concatenate([jnp.where(first, x, y), jnp.where(first, y, x)], 0)

    def gather(wide, pack):
        got = swap(wide, "gene", 1)
        parts = [swap(pack, "gene", bits) for bits in stages(1, n_gene)[0]]
        near = parts[0]
        whole = pack
        for more in parts:
            whole = whole + more
        if n_gene > 4:
            whole = exchange_sum(whole, "gene", 4)
        return got, near, whole

    def cross_of(wide, got, pack, near, size):
        own_size = size * weight_of(pack[0:1])
        near_size = size * weight_of(near[0:1])
        cross = (wide[:k] + got[:k]) - own_size * wide[k : 2 * k] - near_size * got[k : 2 * k]
        bit = 2
        while bit < n_gene:
            cross = cross + swap(cross, "gene", bit)
            bit *= 2
        return cross, own_size

    def gradient(counts_in, factors, loads, own, library):
        first = library is None
        pace = None
        if first:
            pack, high, low, counts_in, factors, loads, pace = forward_first(
                counts_in, factors, loads, step[None], scale
            )
        else:
            pack, high, low = forward_again(factors, loads, scale)
        wide = products(counts_in, loads, high, low, scale)
        got, near, whole = gather(wide, pack)
        data = data_part(counts_in, factors, scale)
        library = whole[1:2] if first else library
        size = library / whole[0:1]
        cross, own_size = cross_of(wide, got, pack, near, size)
        send = part(at_send, factors, own_size, data, high, low, scale)
        back = swap(send, "cell", 1)
        kept = part(at_own, factors, own_size, data, high, low, scale)
        total = exchange_sum(back + kept, "cell", 2)
        ard = (genes_total + 2.0) / (whole[2, :k] + 2.0)
        own = mine(loads) if first else own
        grad_v = total - mine(ard[:, None]) * own
        return cross - factors, grad_v, library, size, counts_in, factors, own, pace

    mom_v = mine(loading_momenta)
    grad_u, grad_v, library, size, counts_small, factors, own, pace = gradient(
        counts, cell_factors, loadings, None, None
    )
    full = jnp.reshape(pace, (k, 1))
    full_own = mine(full)
    half, half_own = 0.5 * full, 0.5 * full_own
    mom_u = cell_momenta + half * grad_u
    mom_v = mom_v + half_own * grad_v
    factors = factors + full * mom_u
    own = own + full_own * mom_v
    loads = join(own)
    grad_u, grad_v, library, size, *_ = gradient(
        counts_small, factors, loads, own, library
    )
    rates = rates_of(factors, loads, size, scale)
    mom_u = mom_u + half * grad_u
    own_mom = mom_v + half_own * grad_v
    mom_u, mom_v = finish(at_own, own_mom, swap(own_mom, "cell", 1), mom_u)
    return (factors, loads, mom_u, mom_v, rates)


def solution(mesh):
    placed = (
        P("cell", "gene"),
        P(None, "cell"),
        P(None, "gene"),
        P(None, "cell"),
        P(None, "gene"),
        P(),
    )
    return jax.shard_map(
        local,
        mesh=mesh,
        in_specs=placed,
        out_specs=(
            P(None, "cell"),
            P(None, "gene"),
            P(None, "cell"),
            P(None, "gene"),
            P("cell", "gene"),
        ),
        check_vma=False,
    )
```

```python
import functools

import jax
import jax.numpy as jnp
from jax import lax
from jax.experimental import pallas as pl
from jax.experimental.pallas import tpu as pltpu
from jax.sharding import PartitionSpec as P


PARAMS = pltpu.CompilerParams(vmem_limit_bytes=24 * 1024 * 1024)
PIECES = 4
FLOOR = 2.0**-100
VMEM = pl.BlockSpec(memory_space=pltpu.VMEM)
HBM = pl.BlockSpec(memory_space=pltpu.HBM)
SMEM = pl.BlockSpec(memory_space=pltpu.SMEM)
NT = (((1,), (1,)), ((), ()))
TN = (((0,), (0,)), ((), ()))
NN = (((1,), (0,)), ((), ()))


def dot(a, b, dims):
    return lax.dot_general(a, b, dims, preferred_element_type=jnp.float32)


def split(x):
    high = x.astype(jnp.bfloat16)
    return high, (x - high.astype(jnp.float32)).astype(jnp.bfloat16)


def weight_of(total):
    return jnp.clip(0.25 * total, FLOOR, 2.0**126)


def forward_math(scale, u, v, pack_ref, high_ref, low_ref):
    u_high, u_low = split(u * scale)
    v_high, v_low = split(v)
    linear = dot(
        jnp.concatenate([v_high, v_low, v_high, v_low], 0),
        jnp.concatenate([u_high, u_high, u_low, u_low], 0),
        TN,
    )
    expo = jnp.exp(linear)
    total = jnp.sum(expo, axis=0, keepdims=True)
    p_high, p_low = split(expo * (1.0 / weight_of(total)))
    high_ref[...] = p_high
    low_ref[...] = p_low
    ones = jnp.ones((16, v.shape[1]), jnp.bfloat16)
    s_high, s_low = split(v * v)
    squares = dot(ones, s_high, NT) + dot(ones, s_low, NT)
    pack_ref[...] = jnp.zeros(pack_ref.shape, jnp.float32)
    pack_ref[0:1, :] = total
    pack_ref[2:3, 0 : v.shape[0]] = squares[0:1]


def first_kernel(scale, counts_hbm, u_hbm, v_hbm, step_hbm, pack_ref, high_ref, low_ref, small_ref,
                 u_ref, v_ref, step_ref, counts_ref, sems):
    copies = [
        pltpu.make_async_copy(v_hbm, v_ref, sems.at[0]),
        pltpu.make_async_copy(u_hbm, u_ref, sems.at[1]),
    ]
    pieces = sems.shape[0] - 3
    rows = counts_ref.shape[0] // pieces
    for i in range(pieces):
        at = pl.ds(i * rows, rows)
        copies.append(
            pltpu.make_async_copy(counts_hbm.at[at, :], counts_ref.at[at, :], sems.at[2 + i])
        )
    copies.append(pltpu.make_async_copy(step_hbm, step_ref, sems.at[2 + pieces]))
    for copy in copies:
        copy.start()
    copies[0].wait()
    copies[1].wait()
    forward_math(scale, u_ref[...], v_ref[...], pack_ref, high_ref, low_ref)
    for copy in copies[2:]:
        copy.wait()
    small = counts_ref[...].astype(jnp.float32).astype(jnp.bfloat16)
    small_ref[...] = small
    ones = jnp.ones((16, small.shape[1]), jnp.bfloat16)
    pack_ref[1:2, :] = dot(ones, small, NT)[0:1]


def again_kernel(scale, u_ref, v_ref, *outs):
    forward_math(scale, u_ref[...], v_ref[...], *outs)


def forward_first(counts, u, v, step, scale):
    cells, genes = counts.shape
    shapes = [
        jax.ShapeDtypeStruct((8, cells), jnp.float32),
        jax.ShapeDtypeStruct((genes, cells), jnp.bfloat16),
        jax.ShapeDtypeStruct((genes, cells), jnp.bfloat16),
        jax.ShapeDtypeStruct((cells, genes), jnp.bfloat16),
        jax.ShapeDtypeStruct(u.shape, u.dtype),
        jax.ShapeDtypeStruct(v.shape, v.dtype),
        jax.ShapeDtypeStruct(step.shape, step.dtype),
    ]
    return pl.pallas_call(
        functools.partial(first_kernel, scale),
        out_shape=shapes,
        in_specs=[HBM] * 4,
        out_specs=[VMEM] * len(shapes),
        scratch_shapes=[
            pltpu.VMEM((cells, genes), counts.dtype),
            pltpu.SemaphoreType.DMA((3 + PIECES,)),
        ],
        name="forward_first",
        compiler_params=PARAMS,
    )(*(pltpu.with_memory_space_constraint(x, pltpu.HBM) for x in (counts, u, v, step)))


def forward_again(u, v, scale):
    cells, genes = u.shape[1], v.shape[1]
    shapes = [
        jax.ShapeDtypeStruct((8, cells), jnp.float32),
        jax.ShapeDtypeStruct((genes, cells), jnp.bfloat16),
        jax.ShapeDtypeStruct((genes, cells), jnp.bfloat16),
    ]
    return pl.pallas_call(
        functools.partial(again_kernel, scale),
        out_shape=shapes,
        in_specs=[VMEM] * 2,
        out_specs=[VMEM] * len(shapes),
        name="forward_again",
        compiler_params=PARAMS,
    )(u, v)


def products_kernel(scale, counts_ref, v_ref, high_ref, low_ref, out_ref):
    k = v_ref.shape[0]
    w_high, w_low = split(v_ref[...] * scale)
    both = jnp.concatenate([w_high, w_low], 0)
    data = dot(both, counts_ref[...], NT)
    mean = dot(both, high_ref[...], NN)
    out_ref[0:k, :] = data[:k] + data[k:]
    out_ref[k:, :] = mean[:k] + mean[k:] + dot(w_high, low_ref[...], NN)


def products(counts, v, high, low, scale):
    return pl.pallas_call(
        functools.partial(products_kernel, scale),
        out_shape=jax.ShapeDtypeStruct((2 * v.shape[0], counts.shape[0]), jnp.float32),
        in_specs=[VMEM] * 4,
        out_specs=VMEM,
        name="products",
        compiler_params=PARAMS,
    )(counts, v, high, low)


def rates_kernel(scale, u_ref, v_ref, size_ref, out_ref):
    u_high, u_low = split(u_ref[...] * scale)
    v_high, v_low = split(v_ref[...])
    linear = dot(
        jnp.concatenate([u_high, u_high, u_low, u_low], 0),
        jnp.concatenate([v_high, v_low, v_high, v_low], 0),
        TN,
    )
    log = jnp.log(size_ref[...])
    log_high, log_low = split(log)
    log_least = (log - log_high.astype(jnp.float32) - log_low.astype(jnp.float32)).astype(
        jnp.bfloat16
    )
    row = lax.broadcasted_iota(jnp.int32, (16, log.shape[1]), 0)
    terms = jnp.zeros((16, log.shape[1]), jnp.float32)
    for i, term in enumerate((log_high, log_low, log_least)):
        terms = jnp.where(row == i, term.astype(jnp.float32), terms)
    ones = jnp.ones((16, v_ref.shape[1]), jnp.bfloat16)
    shift = dot(terms.astype(jnp.bfloat16), ones, TN)
    out_ref[...] = (linear + shift).astype(jnp.bfloat16)


def rates_of(u, v, size, scale):
    return pl.pallas_call(
        functools.partial(rates_kernel, scale),
        out_shape=jax.ShapeDtypeStruct((u.shape[1], v.shape[1]), jnp.bfloat16),
        in_specs=[VMEM] * 3,
        out_specs=VMEM,
        name="rates",
        compiler_params=PARAMS,
    )(u, v, size)


def data_kernel(scale, counts_ref, u_ref, high_ref, low_ref, out_ref, high_out, low_out):
    k = u_ref.shape[0]
    u_high, u_low = split(u_ref[...] * scale)
    both = dot(jnp.concatenate([u_high, u_low], 0), counts_ref[...], NN)
    out_ref[...] = both[:k] + both[k:]
    high_out[...] = high_ref[...].T
    low_out[...] = low_ref[...].T


def data_part(counts, u, high, low, scale):
    return pl.pallas_call(
        functools.partial(data_kernel, scale),
        out_shape=(
            jax.ShapeDtypeStruct((u.shape[0], counts.shape[1]), jnp.float32),
            jax.ShapeDtypeStruct(counts.shape, high.dtype),
            jax.ShapeDtypeStruct(counts.shape, low.dtype),
        ),
        in_specs=[VMEM] * 4,
        out_specs=(VMEM,) * 3,
        name="data_part",
        compiler_params=PARAMS,
    )(counts, u, high, low)


def part_kernel(scale, at_ref, u_ref, size_ref, data_ref, high_ref, low_ref, out_ref):
    hk = out_ref.shape[0]
    rows = pl.ds(pl.multiple_of(at_ref[0], hk), hk)
    u_high, u_low = split(u_ref[rows, :] * size_ref[...] * scale)
    both = dot(jnp.concatenate([u_high, u_low], 0), high_ref[...], NN)
    rest = dot(u_high, low_ref[...], NN)
    out_ref[...] = data_ref[rows, :] - (both[:hk] + both[hk:] + rest)


def part(at, u, size, data, high, low, scale):
    return pl.pallas_call(
        functools.partial(part_kernel, scale),
        out_shape=jax.ShapeDtypeStruct((u.shape[0] // 2, high.shape[1]), jnp.float32),
        in_specs=[SMEM] + [VMEM] * 5,
        out_specs=VMEM,
        compiler_params=PARAMS,
    )(at, u, size, data, high, low)


def finish_kernel(at_ref, own_ref, other_ref, u_ref, u_hbm, v_hbm, sems):
    hk = own_ref.shape[0]
    first = pl.multiple_of(at_ref[0], hk)
    copies = (
        pltpu.make_async_copy(u_ref, u_hbm, sems.at[0]),
        pltpu.make_async_copy(own_ref, v_hbm.at[pl.ds(first, hk), :], sems.at[1]),
        pltpu.make_async_copy(other_ref, v_hbm.at[pl.ds(hk - first, hk), :], sems.at[2]),
    )
    for copy in copies:
        copy.start()
    for copy in copies:
        copy.wait()


def finish(at, own, other, u):
    hk, genes = own.shape
    return pl.pallas_call(
        finish_kernel,
        out_shape=(
            jax.ShapeDtypeStruct(u.shape, u.dtype),
            jax.ShapeDtypeStruct((2 * hk, genes), own.dtype),
        ),
        in_specs=[SMEM] + [VMEM] * 3,
        out_specs=(HBM, HBM),
        scratch_shapes=[pltpu.SemaphoreType.DMA((3,))],
        name="finish",
        compiler_params=PARAMS,
    )(at, own, other, u)


def swap(x, axis, bits):
    n = lax.axis_size(axis)
    return lax.ppermute(x, axis, [(j, j ^ bits) for j in range(n)])


def stages(lo, n):
    out = []
    bit = lo
    while bit < n:
        out.append([bit, 2 * bit, 3 * bit] if 4 * bit <= n else [bit])
        bit *= 4
    return out


def exchange_sum(x, axis, lo):
    for group in stages(lo, lax.axis_size(axis)):
        parts = [swap(x, axis, bits) for bits in group]
        for got in parts:
            x = x + got
    return x


def local(counts, cell_factors, loadings, cell_momenta, loading_momenta, step):
    k, _ = cell_factors.shape
    scale = 1.0 / k**0.5
    n_gene = lax.axis_size("gene")
    genes_total = jnp.float32(loadings.shape[1] * n_gene)
    hk = k // 2
    side = lax.axis_index("cell") % 2
    at_own = jnp.reshape(side * hk, (1,)).astype(jnp.int32)
    at_send = hk - at_own

    def mine(x):
        return lax.dynamic_slice_in_dim(x, side * hk, hk, 0)

    def join(x):
        y = swap(x, "cell", 1)
        first = side == 0
        return jnp.concatenate([jnp.where(first, x, y), jnp.where(first, y, x)], 0)

    def gather(wide, pack):
        got = swap(wide, "gene", 1)
        parts = [swap(pack, "gene", bits) for bits in stages(1, n_gene)[0]]
        near = parts[0]
        whole = pack
        for more in parts:
            whole = whole + more
        if n_gene > 4:
            whole = exchange_sum(whole, "gene", 4)
        return got, near, whole

    def cross_of(wide, got, pack, near, size):
        own_size = size * weight_of(pack[0:1])
        near_size = size * weight_of(near[0:1])
        cross = (wide[:k] + got[:k]) - own_size * wide[k : 2 * k] - near_size * got[k : 2 * k]
        bit = 2
        while bit < n_gene:
            cross = cross + swap(cross, "gene", bit)
            bit *= 2
        return cross, own_size

    def gradient(counts_in, factors, loads, own, library):
        first = library is None
        pace = None
        if first:
            pack, high, low, counts_in, factors, loads, pace = forward_first(
                counts_in, factors, loads, step[None], scale
            )
        else:
            pack, high, low = forward_again(factors, loads, scale)
        wide = products(counts_in, loads, high, low, scale)
        got, near, whole = gather(wide, pack)
        data, high, low = data_part(counts_in, factors, high, low, scale)
        library = whole[1:2] if first else library
        size = library / whole[0:1]
        cross, own_size = cross_of(wide, got, pack, near, size)
        send = part(at_send, factors, own_size, data, high, low, scale)
        back = swap(send, "cell", 1)
        kept = part(at_own, factors, own_size, data, high, low, scale)
        total = exchange_sum(back + kept, "cell", 2)
        ard = (genes_total + 2.0) / (whole[2, :k] + 2.0)
        own = mine(loads) if first else own
        grad_v = total - mine(ard[:, None]) * own
        return cross - factors, grad_v, library, size, counts_in, factors, own, pace

    mom_v = mine(loading_momenta)
    grad_u, grad_v, library, size, counts_small, factors, own, pace = gradient(
        counts, cell_factors, loadings, None, None
    )
    full = jnp.reshape(pace, (k, 1))
    full_own = mine(full)
    half, half_own = 0.5 * full, 0.5 * full_own
    mom_u = cell_momenta + half * grad_u
    mom_v = mom_v + half_own * grad_v
    factors = factors + full * mom_u
    own = own + full_own * mom_v
    loads = join(own)
    grad_u, grad_v, library, size, *_ = gradient(
        counts_small, factors, loads, own, library
    )
    rates = rates_of(factors, loads, size, scale)
    mom_u = mom_u + half * grad_u
    own_mom = mom_v + half_own * grad_v
    mom_u, mom_v = finish(at_own, own_mom, swap(own_mom, "cell", 1), mom_u)
    return (factors, loads, mom_u, mom_v, rates)


def solution(mesh):
    placed = (
        P("cell", "gene"),
        P(None, "cell"),
        P(None, "gene"),
        P(None, "cell"),
        P(None, "gene"),
        P(),
    )
    return jax.shard_map(
        local,
        mesh=mesh,
        in_specs=placed,
        out_specs=(
            P(None, "cell"),
            P(None, "gene"),
            P(None, "cell"),
            P(None, "gene"),
            P("cell", "gene"),
        ),
        check_vma=False,
    )
```

```python
import functools

import jax
import jax.numpy as jnp
from jax import lax
from jax.experimental import pallas as pl
from jax.experimental.pallas import tpu as pltpu
from jax.sharding import PartitionSpec as P


PARAMS = pltpu.CompilerParams(vmem_limit_bytes=24 * 1024 * 1024)
PIECES = 4
FLOOR = 2.0**-100
VMEM = pl.BlockSpec(memory_space=pltpu.VMEM)
HBM = pl.BlockSpec(memory_space=pltpu.HBM)
SMEM = pl.BlockSpec(memory_space=pltpu.SMEM)
NT = (((1,), (1,)), ((), ()))
TN = (((0,), (0,)), ((), ()))
NN = (((1,), (0,)), ((), ()))


def dot(a, b, dims):
    return lax.dot_general(a, b, dims, preferred_element_type=jnp.float32)


def split(x):
    high = x.astype(jnp.bfloat16)
    return high, (x - high.astype(jnp.float32)).astype(jnp.bfloat16)


def weight_of(total):
    return jnp.clip(0.25 * total, FLOOR, 2.0**126)


def forward_math(scale, u, v, pack_ref, high_ref, low_ref):
    u_high, u_low = split(u * scale)
    v_high, v_low = split(v)
    linear = dot(
        jnp.concatenate([v_high, v_low, v_high, v_low], 0),
        jnp.concatenate([u_high, u_high, u_low, u_low], 0),
        TN,
    )
    expo = jnp.exp(linear)
    total = jnp.sum(expo, axis=0, keepdims=True)
    p_high, p_low = split(expo * (1.0 / weight_of(total)))
    high_ref[...] = p_high
    low_ref[...] = p_low
    ones = jnp.ones((16, v.shape[1]), jnp.bfloat16)
    s_high, s_low = split(v * v)
    squares = dot(ones, s_high, NT) + dot(ones, s_low, NT)
    pack_ref[...] = jnp.zeros(pack_ref.shape, jnp.float32)
    pack_ref[0:1, :] = total
    pack_ref[2:3, 0 : v.shape[0]] = squares[0:1]


def first_kernel(scale, counts_hbm, u_hbm, v_hbm, step_hbm, pack_ref, high_ref, low_ref, small_ref,
                 u_ref, v_ref, step_ref, counts_ref, sems):
    copies = [
        pltpu.make_async_copy(v_hbm, v_ref, sems.at[0]),
        pltpu.make_async_copy(u_hbm, u_ref, sems.at[1]),
    ]
    pieces = sems.shape[0] - 3
    rows = counts_ref.shape[0] // pieces
    for i in range(pieces):
        at = pl.ds(i * rows, rows)
        copies.append(
            pltpu.make_async_copy(counts_hbm.at[at, :], counts_ref.at[at, :], sems.at[2 + i])
        )
    copies.append(pltpu.make_async_copy(step_hbm, step_ref, sems.at[2 + pieces]))
    for copy in copies:
        copy.start()
    copies[0].wait()
    copies[1].wait()
    forward_math(scale, u_ref[...], v_ref[...], pack_ref, high_ref, low_ref)
    for copy in copies[2:]:
        copy.wait()
    small = counts_ref[...].astype(jnp.float32).astype(jnp.bfloat16)
    small_ref[...] = small
    ones = jnp.ones((16, small.shape[1]), jnp.bfloat16)
    pack_ref[1:2, :] = dot(ones, small, NT)[0:1]


def again_kernel(scale, u_ref, v_ref, *outs):
    forward_math(scale, u_ref[...], v_ref[...], *outs)


def forward_first(counts, u, v, step, scale):
    cells, genes = counts.shape
    shapes = [
        jax.ShapeDtypeStruct((8, cells), jnp.float32),
        jax.ShapeDtypeStruct((genes, cells), jnp.bfloat16),
        jax.ShapeDtypeStruct((genes, cells), jnp.bfloat16),
        jax.ShapeDtypeStruct((cells, genes), jnp.bfloat16),
        jax.ShapeDtypeStruct(u.shape, u.dtype),
        jax.ShapeDtypeStruct(v.shape, v.dtype),
        jax.ShapeDtypeStruct(step.shape, step.dtype),
    ]
    return pl.pallas_call(
        functools.partial(first_kernel, scale),
        out_shape=shapes,
        in_specs=[HBM] * 4,
        out_specs=[VMEM] * len(shapes),
        scratch_shapes=[
            pltpu.VMEM((cells, genes), counts.dtype),
            pltpu.SemaphoreType.DMA((3 + PIECES,)),
        ],
        name="forward_first",
        compiler_params=PARAMS,
    )(*(pltpu.with_memory_space_constraint(x, pltpu.HBM) for x in (counts, u, v, step)))


def forward_again(u, v, scale):
    cells, genes = u.shape[1], v.shape[1]
    shapes = [
        jax.ShapeDtypeStruct((8, cells), jnp.float32),
        jax.ShapeDtypeStruct((genes, cells), jnp.bfloat16),
        jax.ShapeDtypeStruct((genes, cells), jnp.bfloat16),
    ]
    return pl.pallas_call(
        functools.partial(again_kernel, scale),
        out_shape=shapes,
        in_specs=[VMEM] * 2,
        out_specs=[VMEM] * len(shapes),
        name="forward_again",
        compiler_params=PARAMS,
    )(u, v)


def products_kernel(scale, counts_ref, v_ref, high_ref, low_ref, out_ref):
    k = v_ref.shape[0]
    w_high, w_low = split(v_ref[...] * scale)
    both = jnp.concatenate([w_high, w_low], 0)
    data = dot(both, counts_ref[...], NT)
    mean = dot(both, high_ref[...], NN)
    out_ref[0:k, :] = data[:k] + data[k:]
    out_ref[k:, :] = mean[:k] + mean[k:] + dot(w_high, low_ref[...], NN)


def products(counts, v, high, low, scale):
    return pl.pallas_call(
        functools.partial(products_kernel, scale),
        out_shape=jax.ShapeDtypeStruct((2 * v.shape[0], counts.shape[0]), jnp.float32),
        in_specs=[VMEM] * 4,
        out_specs=VMEM,
        name="products",
        compiler_params=PARAMS,
    )(counts, v, high, low)


def rates_kernel(scale, u_ref, v_ref, size_ref, out_ref):
    u_high, u_low = split(u_ref[...] * scale)
    v_high, v_low = split(v_ref[...])
    linear = dot(
        jnp.concatenate([u_high, u_high, u_low, u_low], 0),
        jnp.concatenate([v_high, v_low, v_high, v_low], 0),
        TN,
    )
    log = jnp.log(size_ref[...])
    log_high, log_low = split(log)
    log_least = (log - log_high.astype(jnp.float32) - log_low.astype(jnp.float32)).astype(
        jnp.bfloat16
    )
    row = lax.broadcasted_iota(jnp.int32, (16, log.shape[1]), 0)
    terms = jnp.zeros((16, log.shape[1]), jnp.float32)
    for i, term in enumerate((log_high, log_low, log_least)):
        terms = jnp.where(row == i, term.astype(jnp.float32), terms)
    ones = jnp.ones((16, v_ref.shape[1]), jnp.bfloat16)
    shift = dot(terms.astype(jnp.bfloat16), ones, TN)
    out_ref[...] = (linear + shift).astype(jnp.bfloat16)


def rates_of(u, v, size, scale):
    return pl.pallas_call(
        functools.partial(rates_kernel, scale),
        out_shape=jax.ShapeDtypeStruct((u.shape[1], v.shape[1]), jnp.bfloat16),
        in_specs=[VMEM] * 3,
        out_specs=VMEM,
        name="rates",
        compiler_params=PARAMS,
    )(u, v, size)


def data_kernel(scale, counts_ref, u_ref, high_ref, low_ref, out_ref, both_out):
    k = u_ref.shape[0]
    u_high, u_low = split(u_ref[...] * scale)
    both = dot(jnp.concatenate([u_high, u_low], 0), counts_ref[...], NN)
    out_ref[...] = both[:k] + both[k:]
    cells = counts_ref.shape[0]
    both_out[0:cells, :] = high_ref[...].T
    both_out[cells:, :] = low_ref[...].T


def data_part(counts, u, high, low, scale):
    return pl.pallas_call(
        functools.partial(data_kernel, scale),
        out_shape=(
            jax.ShapeDtypeStruct((u.shape[0], counts.shape[1]), jnp.float32),
            jax.ShapeDtypeStruct((2 * counts.shape[0], counts.shape[1]), high.dtype),
        ),
        in_specs=[VMEM] * 4,
        out_specs=(VMEM,) * 2,
        name="data_part",
        compiler_params=PARAMS,
    )(counts, u, high, low)


def part_kernel(scale, at_ref, u_ref, size_ref, data_ref, probs_ref, out_ref):
    hk = out_ref.shape[0]
    rows = pl.ds(pl.multiple_of(at_ref[0], hk), hk)
    u_high, u_low = split(u_ref[rows, :] * size_ref[...] * scale)
    u_both = jnp.concatenate([u_high, u_low], 0)
    both = dot(jnp.concatenate([u_both, u_both], 1), probs_ref[...], NN)
    out_ref[...] = data_ref[rows, :] - (both[:hk] + both[hk:])


def part(at, u, size, data, probs, scale):
    return pl.pallas_call(
        functools.partial(part_kernel, scale),
        out_shape=jax.ShapeDtypeStruct((u.shape[0] // 2, probs.shape[1]), jnp.float32),
        in_specs=[SMEM] + [VMEM] * 4,
        out_specs=VMEM,
        compiler_params=PARAMS,
    )(at, u, size, data, probs)


def finish_kernel(at_ref, own_ref, other_ref, u_ref, u_hbm, v_hbm, sems):
    hk = own_ref.shape[0]
    first = pl.multiple_of(at_ref[0], hk)
    copies = (
        pltpu.make_async_copy(u_ref, u_hbm, sems.at[0]),
        pltpu.make_async_copy(own_ref, v_hbm.at[pl.ds(first, hk), :], sems.at[1]),
        pltpu.make_async_copy(other_ref, v_hbm.at[pl.ds(hk - first, hk), :], sems.at[2]),
    )
    for copy in copies:
        copy.start()
    for copy in copies:
        copy.wait()


def finish(at, own, other, u):
    hk, genes = own.shape
    return pl.pallas_call(
        finish_kernel,
        out_shape=(
            jax.ShapeDtypeStruct(u.shape, u.dtype),
            jax.ShapeDtypeStruct((2 * hk, genes), own.dtype),
        ),
        in_specs=[SMEM] + [VMEM] * 3,
        out_specs=(HBM, HBM),
        scratch_shapes=[pltpu.SemaphoreType.DMA((3,))],
        name="finish",
        compiler_params=PARAMS,
    )(at, own, other, u)


def swap(x, axis, bits):
    n = lax.axis_size(axis)
    return lax.ppermute(x, axis, [(j, j ^ bits) for j in range(n)])


def stages(lo, n):
    out = []
    bit = lo
    while bit < n:
        out.append([bit, 2 * bit, 3 * bit] if 4 * bit <= n else [bit])
        bit *= 4
    return out


def exchange_sum(x, axis, lo):
    for group in stages(lo, lax.axis_size(axis)):
        parts = [swap(x, axis, bits) for bits in group]
        for got in parts:
            x = x + got
    return x


def local(counts, cell_factors, loadings, cell_momenta, loading_momenta, step):
    k, _ = cell_factors.shape
    scale = 1.0 / k**0.5
    n_gene = lax.axis_size("gene")
    genes_total = jnp.float32(loadings.shape[1] * n_gene)
    hk = k // 2
    side = lax.axis_index("cell") % 2
    at_own = jnp.reshape(side * hk, (1,)).astype(jnp.int32)
    at_send = hk - at_own

    def mine(x):
        return lax.dynamic_slice_in_dim(x, side * hk, hk, 0)

    def join(x):
        y = swap(x, "cell", 1)
        first = side == 0
        return jnp.concatenate([jnp.where(first, x, y), jnp.where(first, y, x)], 0)

    def gather(wide, pack):
        got = swap(wide, "gene", 1)
        parts = [swap(pack, "gene", bits) for bits in stages(1, n_gene)[0]]
        near = parts[0]
        whole = pack
        for more in parts:
            whole = whole + more
        if n_gene > 4:
            whole = exchange_sum(whole, "gene", 4)
        return got, near, whole

    def cross_of(wide, got, pack, near, size):
        own_size = size * weight_of(pack[0:1])
        near_size = size * weight_of(near[0:1])
        cross = (wide[:k] + got[:k]) - own_size * wide[k : 2 * k] - near_size * got[k : 2 * k]
        bit = 2
        while bit < n_gene:
            cross = cross + swap(cross, "gene", bit)
            bit *= 2
        return cross, own_size

    def gradient(counts_in, factors, loads, own, library):
        first = library is None
        pace = None
        if first:
            pack, high, low, counts_in, factors, loads, pace = forward_first(
                counts_in, factors, loads, step[None], scale
            )
        else:
            pack, high, low = forward_again(factors, loads, scale)
        wide = products(counts_in, loads, high, low, scale)
        got, near, whole = gather(wide, pack)
        data, probs = data_part(counts_in, factors, high, low, scale)
        library = whole[1:2] if first else library
        size = library / whole[0:1]
        cross, own_size = cross_of(wide, got, pack, near, size)
        send = part(at_send, factors, own_size, data, probs, scale)
        back = swap(send, "cell", 1)
        kept = part(at_own, factors, own_size, data, probs, scale)
        total = exchange_sum(back + kept, "cell", 2)
        ard = (genes_total + 2.0) / (whole[2, :k] + 2.0)
        own = mine(loads) if first else own
        grad_v = total - mine(ard[:, None]) * own
        return cross - factors, grad_v, library, size, counts_in, factors, own, pace

    mom_v = mine(loading_momenta)
    grad_u, grad_v, library, size, counts_small, factors, own, pace = gradient(
        counts, cell_factors, loadings, None, None
    )
    full = jnp.reshape(pace, (k, 1))
    full_own = mine(full)
    half, half_own = 0.5 * full, 0.5 * full_own
    mom_u = cell_momenta + half * grad_u
    mom_v = mom_v + half_own * grad_v
    factors = factors + full * mom_u
    own = own + full_own * mom_v
    loads = join(own)
    grad_u, grad_v, library, size, *_ = gradient(
        counts_small, factors, loads, own, library
    )
    rates = rates_of(factors, loads, size, scale)
    mom_u = mom_u + half * grad_u
    own_mom = mom_v + half_own * grad_v
    mom_u, mom_v = finish(at_own, own_mom, swap(own_mom, "cell", 1), mom_u)
    return (factors, loads, mom_u, mom_v, rates)


def solution(mesh):
    placed = (
        P("cell", "gene"),
        P(None, "cell"),
        P(None, "gene"),
        P(None, "cell"),
        P(None, "gene"),
        P(),
    )
    return jax.shard_map(
        local,
        mesh=mesh,
        in_specs=placed,
        out_specs=(
            P(None, "cell"),
            P(None, "gene"),
            P(None, "cell"),
            P(None, "gene"),
            P("cell", "gene"),
        ),
        check_vma=False,
    )
```
